256 devices in a mesh: rows: 64 (over z, y, core), src: 4 (over x).
Axes of the slice: x: 4, y: 4, z: 8, core: 2. Of those that a mesh axis runs over, the one named last changes fastest.
Arguments:
- misfit: float32 [256, 64, 1024], P('rows', 'src'), may hold values from -6 to 6
- forward_fields: bfloat16 [256, 64, 1024], P('rows', 'src'), may hold values from -6 to 6
- contrast: float32 [256, 1024], P('rows'), may hold values from 0.2 to 0.6
- u_factors: bfloat16 [256, 16, 96, 1024], P('rows'), may hold values from -0.1875 to 0.1875
- v_factors: bfloat16 [256, 16, 96, 1024], P('rows'), may hold values from -0.1796875 to 0.1796875
- ranks: int32 [256, 16], P('rows'), may hold values from 32 to 96
- tile_cols: int32 [256, 16], replicated, may hold values from 0 to 255, as said below
- owner_slot: int32 [256], replicated, may hold values from 0 to 255, as said below
Outputs:
- adjoint_field: float32 [256, 64, 1024], P('rows', 'src')
- gradient: float32 [256, 1024], P('rows')
The draws below stay inside these ranges and needn't reach their ends.
Inputs may be any that keep to these rules, and one draw needn't show every extreme that they name: The 16 entries of each row of tile_cols differ. With a tile's receiving device taken as owner_slot[tile_cols[s, k]] // 4 and its sending device as s // 4, at most 1 tiles of one sending device go to one receiving device, and every sending device sends exactly 1 to some receiving device. Each block of unknowns has exactly one slot: owner_slot is a permutation.
All inputs are finite; a program needn't handle non-finite values.
Results may differ from the reference program's by a relative error of at most 0.005.
Values may be sent and summed in bfloat16 or wider, within the bound.
A program may use at most 192 MiB of HBM per device.

```python
import math
import jax
import jax.numpy as jnp
from jax import lax

B = 1024
K = 16
RMAX = 96
R_DEV = 4
APPS = 4
NT = 256
S = 64


def route_helper(key):
    devices = NT // R_DEV
    keys = jax.random.split(jax.random.fold_in(key, 11), devices)
    orders = jax.vmap(lambda single: jax.random.permutation(single, devices))(keys).astype(jnp.int32)
    position = jnp.arange(R_DEV, dtype=jnp.int32)[:, None] * K + jnp.arange(K, dtype=jnp.int32)[None, :]
    wraps = position // devices
    reach = orders[:, position % devices]
    offset = jax.random.randint(jax.random.fold_in(key, 12), (devices, devices), 0, R_DEV).astype(jnp.int32)
    shifted = jnp.take_along_axis(offset, reach.reshape(devices, R_DEV * K), axis=1).reshape(devices, R_DEV, K)
    local = (wraps[None, :, :] + shifted) % R_DEV
    slots = (reach * R_DEV + local).reshape(NT, K)
    owner = jax.random.permutation(jax.random.fold_in(key, 13), NT).astype(jnp.int32)
    inverse = jnp.zeros((NT,), jnp.int32).at[owner].set(jnp.arange(NT, dtype=jnp.int32))
    return (inverse[slots], owner)


def draw_tile_cols(key, part):
    return route_helper(key)[0].astype(jnp.int32)


def draw_owner_slot(key, part):
    return route_helper(key)[1].astype(jnp.int32)


def touch_ends(values, key, smallest, high):
    longest = values.shape.index(max(values.shape))
    spots = []
    for shift in (0, 1):
        where = [jax.random.randint(jax.random.fold_in(key, axis), (), 0, length) for axis, length in enumerate(values.shape)]
        where[longest] = (where[longest] + shift) % values.shape[longest]
        spots.append(tuple(where))
    return values.at[spots[0]].set(smallest).at[spots[1]].set(high)


def block_levels(rng, shape, shards, least, top_value):
    def one(dim, shards_of):
        steps = jax.random.uniform(jax.random.fold_in(jax.random.fold_in(rng, 6), dim), (shards_of,), jnp.float32, least / len(shards), top_value / len(shards))
        return jnp.repeat(jnp.exp(steps), shape[dim] // shards_of).reshape((-1,) + (1,) * (len(shape) - dim - 1))

    factor_of = one(*shards[0])
    for cut in shards[1:]:
        factor_of = factor_of * one(*cut)
    return factor_of


def centred(stream_key, shape, scale, most, pieces=(), kind=jnp.bfloat16):
    result = scale * jax.random.normal(stream_key, shape, jnp.float32)
    if pieces:
        result = result * block_levels(stream_key, shape, pieces, -0.22, 0.18)
    return jnp.clip(result, -most, most).astype(kind)


def setup_inputs(seed: int = 0) -> dict:
    arg_keys = jax.random.split(jax.random.key(seed), 9)
    misfit = centred(arg_keys[0], (NT, S, B), 1.0, 6.0, ((0, 64), (1, 4)), jnp.float32)
    forward_fields = centred(arg_keys[1], (NT, S, B), 1.0, 6.0, ((0, 64), (1, 4)))
    contrast = jnp.clip(jnp.exp(math.log(0.6) - 1.0986123 * jax.random.uniform(arg_keys[2], (NT, B), jnp.float32) ** block_levels(arg_keys[2], (NT, B), ((0, 64),), -0.2, 0.2)), 0.2, 0.6)
    u_factors = centred(arg_keys[3], (NT, K, RMAX, B), B ** -0.5, 0.1875, ((0, 64),))
    v_factors = centred(arg_keys[4], (NT, K, RMAX, B), 0.03, 0.1796875, ((0, 64),))
    ranks = touch_ends(jax.random.randint(arg_keys[5], (NT, K), RMAX // 3, RMAX + 1), jax.random.fold_in(arg_keys[5], 1), RMAX // 3, RMAX).astype(jnp.int32)
    tile_cols = draw_tile_cols(jax.random.fold_in(arg_keys[8], 71), 0)
    owner_slot = draw_owner_slot(jax.random.fold_in(arg_keys[8], 71), 0)
    return {"misfit": misfit, "forward_fields": forward_fields, "contrast": contrast, "u_factors": u_factors, "v_factors": v_factors, "ranks": ranks, "tile_cols": tile_cols, "owner_slot": owner_slot}


def reference(misfit, forward_fields, contrast, u_factors, v_factors, ranks, tile_cols, owner_slot):
    target = owner_slot[tile_cols].astype(jnp.int32)
    keep = (jnp.arange(RMAX, dtype=jnp.int32)[None, None, :] < ranks[:, :, None]).astype(jnp.float32)
    field = misfit
    for step in range(APPS):
        low = field.astype(jnp.bfloat16)

        def add_row(total, row):
            u_row, v_row, keep_row, low_row, dest = row
            coeff = jnp.einsum('sb,krb->ksr', low_row.astype(jnp.float32), u_row.astype(jnp.float32))
            coeff = (coeff * keep_row[:, None, :]).astype(jnp.bfloat16)
            coeff = lax.optimization_barrier(coeff).astype(jnp.float32)
            terms = jnp.einsum('ksr,krb->ksb', coeff, v_row.astype(jnp.float32))
            return (total.at[dest].add(terms), None)
        total, unused = lax.scan(add_row, jnp.zeros(misfit.shape, jnp.float32), (u_factors, v_factors, keep, low, target))
        field = misfit + contrast[:, None, :] * total
    gradient = lax.optimization_barrier(jnp.sum(forward_fields.astype(jnp.float32) * field, axis=1)) * lax.rsqrt(jnp.float32(S))
    return (field, gradient)
```

```python
import jax
import jax.numpy as jnp
from jax import lax
from jax.experimental import pallas as pl
from jax.experimental.pallas import tpu as pltpu
from jax.sharding import PartitionSpec as P

B = 1024
K = 16
RMAX = 96
APPS = 4
ROWS_DEV = 4
TILES = ROWS_DEV * K
NZ = 8
NY = 4
NM = 8
SRC = 16
PEERS = NZ * NM
NSRC = 4
MESH = pl.DeviceIdType.MESH
CONTRACT_LAST = (((1,), (1,)), ((), ()))
F32 = jnp.float32
BF16 = jnp.bfloat16
CHUNK = 256


def offset_of(k):
    return 4 + (1 - 2 * (k % 2)) * ((k + 1) // 2)


def kernel(
    tab,
    misfit,
    forward,
    contrast,
    onehot,
    u_hbm,
    v_hbm,
    field_ref,
    grad_ref,
    u,
    v,
    low,
    coeff,
    send,
    recv,
    zs,
    zin,
    gbuf,
    load_sem,
    send_sem,
    recv_sem,
    zs_sem,
    zr_sem,
    gs_sem,
    gr_sem,
):
    here = lax.axis_index("rows")
    me_src = lax.axis_index("src")
    z = here // NM
    m = here % NM
    y = m // 2
    c = m % 2

    load_u = pltpu.make_async_copy(u_hbm, u, load_sem.at[0])
    load_v = pltpu.make_async_copy(v_hbm, v, load_sem.at[1])
    load_u.start()
    load_v.start()

    z_up = {"rows": ((z + 1) % NZ) * NM + m}
    z_down = {"rows": ((z + NZ - 1) % NZ) * NM + m}
    peers = []
    for dy in (1, 3, 2, 0):
        for dc in (0, 1):
            if dy or dc:
                peers.append(((y + dy) % NY) * 2 + (c + dc) % 2)
    barrier = pltpu.get_barrier_semaphore()
    for mm in peers:
        pl.semaphore_signal(barrier, inc=1, device_id={"rows": z * NM + mm}, device_id_type=MESH)
    for dev in (z_up, z_down):
        pl.semaphore_signal(barrier, inc=1, device_id=dev, device_id_type=MESH)
    for ds in (1, 2, 3):
        pl.semaphore_signal(
            barrier, inc=1, device_id={"src": (me_src + ds) % NSRC}, device_id_type=MESH
        )

    for p in range(2):
        zin[p, 0] = jnp.zeros((TILES, B), BF16)
        zin[p, 1, 32:64] = jnp.zeros((32, B), BF16)
        zin[p, 2, 0:32] = jnp.zeros((32, B), BF16)
    low[...] = misfit[...].astype(BF16).reshape(ROWS_DEV, SRC, B)
    load_u.wait()
    load_v.wait()
    pl.semaphore_wait(barrier, len(peers) + 2 + NSRC - 1)

    order = peers + [m]
    lane = lax.broadcasted_iota(jnp.int32, (SRC, RMAX), 1)

    def y_copy(par, k, i):
        return pltpu.make_async_remote_copy(
            src_ref=send.at[k, i],
            dst_ref=recv.at[par, k, m],
            send_sem=send_sem.at[k, i],
            recv_sem=recv_sem.at[par, k, m],
            device_id={"rows": z * NM + order[i]},
            device_id_type=MESH,
        )

    def y_arrival(par, k, i):
        return pltpu.make_async_remote_copy(
            src_ref=send.at[k, i],
            dst_ref=recv.at[par, k, order[i]],
            send_sem=send_sem.at[k, i],
            recv_sem=recv_sem.at[par, k, order[i]],
            device_id={"rows": z * NM + order[i]},
            device_id_type=MESH,
        )

    def compute(par, k):
        zt = (z + offset_of(k)) % NZ
        for i in range(NM):
            d = zt * NM + order[i]
            j = tab[0, d]
            acc = lax.dot_general(low[tab[1, d]], u[j], CONTRACT_LAST, preferred_element_type=F32)
            coeff[i] = jnp.where(lane < tab[2, d], acc, 0.0).astype(BF16)
        for i in range(NM):
            d = zt * NM + order[i]
            terms = jnp.dot(coeff[i], v[tab[0, d]], preferred_element_type=F32).astype(BF16)
            if i < NM - 1:
                send[k, i] = terms
                y_copy(par, k, i).start()
            else:
                recv[par, k, m] = terms

    def z_full(par, k):
        return pltpu.make_async_remote_copy(
            src_ref=zs.at[k],
            dst_ref=zin.at[par, k + 2],
            send_sem=zs_sem.at[k],
            recv_sem=zr_sem.at[par, k + 2],
            device_id={"rows": ((z + NZ + 2 * (k % 2) - 1) % NZ) * NM + m},
            device_id_type=MESH,
        )

    def z_first(par, up):
        rows = pl.ds(0, 32) if up else pl.ds(32, 32)
        to = 1 if up else 2
        return pltpu.make_async_remote_copy(
            src_ref=zs.at[0, rows],
            dst_ref=zin.at[par, to, rows],
            send_sem=zs_sem.at[0 if up else 7],
            recv_sem=zr_sem.at[par, to],
            device_id=z_up if up else z_down,
            device_id_type=MESH,
        )

    def slot_sums(par, k, cols):
        got = recv[par, k, :, :, cols].reshape(NM * SRC, CHUNK)
        acc = jnp.dot(onehot[k], got, preferred_element_type=F32)
        return acc + zin[par, k, :, cols].astype(F32)

    def reduce(par, k):
        for i in range(NM - 1):
            y_arrival(par, k, i).wait_recv()

        @pl.when(k == 1)
        def _():
            z_first(par, True).wait_recv()

        @pl.when(k == 2)
        def _():
            z_first(par, False).wait_recv()

        @pl.when(k >= 3)
        def _():
            z_full(par, k - 2).wait_recv()

        @pl.when(k < 7)
        def _():
            for ch in range(B // CHUNK):
                cols = pl.ds(ch * CHUNK, CHUNK)
                zs[k, :, cols] = slot_sums(par, k, cols).astype(BF16)

        @pl.when(k == 0)
        def _():
            z_first(par, True).start()
            z_first(par, False).start()

        @pl.when((k > 0) & (k < 7))
        def _():
            z_full(par, k).start()

    def application(a, carry):
        par = a % 2

        def step(kk, inner):
            @pl.when(kk < NZ)
            def _():
                compute(par, kk)

            @pl.when((kk >= 2) & (kk < NZ + 1))
            def _():
                reduce(par, kk - 2)

            return inner

        lax.fori_loop(0, NZ + 1, step, 0)
        reduce(par, jnp.int32(7))
        z_full(par, 6).wait_recv()
        for ch in range(B // CHUNK):
            cols = pl.ds(ch * CHUNK, CHUNK)
            total = slot_sums(par, 7, cols) + zin[par, 8, :, cols].astype(F32)
            for s in range(ROWS_DEV):
                rows = pl.ds(s * SRC, SRC)
                value = (
                    misfit[rows, cols]
                    + contrast[pl.ds(s, 1), cols] * total[s * SRC : (s + 1) * SRC]
                )
                field_ref[rows, cols] = value
                low[s, :, cols] = value.astype(BF16)

        def drain(k, inner):
            for i in range(NM - 1):
                y_copy(par, k, i).wait_send()
            return inner

        lax.fori_loop(0, NZ, drain, 0)
        z_first(par, True).wait_send()
        z_first(par, False).wait_send()

        def z_drain(k, inner):
            z_full(par, k).wait_send()
            return inner

        lax.fori_loop(1, 7, z_drain, 0)
        return carry

    lax.fori_loop(0, APPS, application, 0)

    for s in range(ROWS_DEV):
        rows = pl.ds(s * SRC, SRC)
        product = forward[rows, :].astype(F32) * field_ref[rows, :]
        gbuf[0, pl.ds(s, 1), :] = jnp.sum(product, axis=0, keepdims=True)

    def g_copy(ds):
        return pltpu.make_async_remote_copy(
            src_ref=gbuf.at[0],
            dst_ref=gbuf.at[ds],
            send_sem=gs_sem.at[ds],
            recv_sem=gr_sem.at[ds],
            device_id={"src": (me_src + ds) % NSRC},
            device_id_type=MESH,
        )

    for ds in (1, 2, 3):
        g_copy(ds).start()
    for ds in (1, 2, 3):
        g_copy(ds).wait()
    even = (gbuf[0] + gbuf[2], gbuf[1] + gbuf[3])
    grad_ref[...] = (even[0] + even[1]) * (NSRC * SRC) ** -0.5


def tables(ranks, tile_cols, owner_slot):
    here = lax.axis_index("rows")
    z, m = here // NM, here % NM
    plane = lax.dynamic_slice_in_dim(tile_cols.reshape(NZ, NM, TILES), z, 1, 0)[0]
    slots = jnp.arange(owner_slot.shape[0], dtype=jnp.int32)
    target = jnp.sum(jnp.where(plane[:, :, None] == slots, owner_slot, 0), axis=2)
    target_dev, local = target // ROWS_DEV, target % ROWS_DEV
    mine = lax.dynamic_index_in_dim(target_dev, m, 0, keepdims=False)
    goes = mine[None, :] == jnp.arange(PEERS, dtype=jnp.int32)[:, None]
    tiles = jnp.arange(TILES, dtype=jnp.int32)
    values = jnp.stack([tiles, tiles // K, ranks.reshape(TILES)])
    tab = jnp.sum(jnp.where(goes[None], values[:, None, :], 0), axis=2)
    ks = jnp.arange(NZ, dtype=jnp.int32)
    dest = ((z + offset_of(ks)) % NZ) * NM + m
    comes = target_dev[None] == dest[:, None, None]
    q = jnp.sum(jnp.where(comes, local[None], 0), axis=2)
    row = jnp.arange(TILES, dtype=jnp.int32)[:, None]
    col = jnp.arange(NM * SRC, dtype=jnp.int32)[None, :]
    same = (row % SRC) == (col % SRC)
    onehot = (jnp.repeat(q, SRC, axis=1)[:, None, :] == (row // SRC)[None]) & same[None]
    return tab.astype(jnp.int32), onehot.astype(BF16)


def per_device(
    misfit, forward_fields, contrast, u_factors, v_factors, ranks, tile_cols, owner_slot
):
    tab, onehot = tables(ranks, tile_cols, owner_slot)
    vmem = pl.BlockSpec(memory_space=pltpu.VMEM)
    hbm = pl.BlockSpec(memory_space=pl.ANY)
    dma = pltpu.SemaphoreType.DMA
    field, gradient = pl.pallas_call(
        kernel,
        out_shape=(
            jax.ShapeDtypeStruct((TILES, B), F32),
            jax.ShapeDtypeStruct((ROWS_DEV, B), F32),
        ),
        in_specs=[pl.BlockSpec(memory_space=pltpu.SMEM), vmem, vmem, vmem, vmem, hbm, hbm],
        out_specs=(vmem, vmem),
        scratch_shapes=[
            pltpu.VMEM((TILES, RMAX, B), BF16),
            pltpu.VMEM((TILES, RMAX, B), BF16),
            pltpu.VMEM((ROWS_DEV, SRC, B), BF16),
            pltpu.VMEM((NM, SRC, RMAX), BF16),
            pltpu.VMEM((NZ, NM - 1, SRC, B), BF16),
            pltpu.VMEM((2, NZ, NM, SRC, B), BF16),
            pltpu.VMEM((7, TILES, B), BF16),
            pltpu.VMEM((2, 9, TILES, B), BF16),
            pltpu.VMEM((NSRC, ROWS_DEV, B), F32),
            dma((2,)),
            dma((NZ, NM - 1)),
            dma((2, NZ, NM)),
            dma((8,)),
            dma((2, 9)),
            dma((NSRC,)),
            dma((NSRC,)),
        ],
        compiler_params=pltpu.CompilerParams(
            collective_id=0, has_side_effects=True, vmem_limit_bytes=58 * 1024 * 1024
        ),
    )(
        tab,
        misfit.reshape(TILES, B),
        forward_fields.reshape(TILES, B),
        contrast,
        onehot,
        u_factors.reshape(TILES, RMAX, B),
        v_factors.reshape(TILES, RMAX, B),
    )
    return field.reshape(ROWS_DEV, SRC, B), gradient


def solution(mesh):
    placed = (
        P("rows", "src", None),
        P("rows", "src", None),
        P("rows", None),
        P("rows", None, None, None),
        P("rows", None, None, None),
        P("rows", None),
        P(),
        P(),
    )
    return jax.shard_map(
        per_device,
        mesh=mesh,
        in_specs=placed,
        out_specs=(P("rows", "src", None), P("rows", None)),
        check_vma=False,
    )
```

```python
import jax
import jax.numpy as jnp
from jax import lax
from jax.experimental import pallas as pl
from jax.experimental.pallas import tpu as pltpu
from jax.sharding import PartitionSpec as P

B = 1024
K = 16
RMAX = 96
APPS = 4
ROWS_DEV = 4
TILES = ROWS_DEV * K
NZ = 8
NY = 4
NM = 8
SRC = 16
PEERS = NZ * NM
NSRC = 4
MESH = pl.DeviceIdType.MESH
CONTRACT_LAST = (((1,), (1,)), ((), ()))
F32 = jnp.float32
BF16 = jnp.bfloat16
CHUNK = 256
HALF = 8
LAG = 2


def offsets_of(p):
    far = 4 - 2 * p + 3 * (p // 2)
    return far, jnp.minimum(p, 1) * (NZ - far)


def kernel(
    tab,
    misfit,
    forward,
    contrast,
    onehot,
    u_hbm,
    v_hbm,
    field_ref,
    grad_ref,
    u,
    v,
    low,
    coeff,
    send,
    recv,
    zs,
    zin,
    own,
    gbuf,
    load_sem,
    send_sem,
    recv_sem,
    zs_sem,
    zr_sem,
    gs_sem,
    gr_sem,
):
    here = lax.axis_index("rows")
    me_src = lax.axis_index("src")
    z = here // NM
    m = here % NM
    y = m // 2
    c = m % 2

    load_u = pltpu.make_async_copy(u_hbm, u, load_sem.at[0])
    load_v = pltpu.make_async_copy(v_hbm, v, load_sem.at[1])
    load_u.start()
    load_v.start()

    def z_dev(dz):
        return {"rows": ((z + NZ + dz) % NZ) * NM + m}

    peers = []
    for dy in (2, 1, 3, 0):
        for dc in (0, 1):
            if dy or dc:
                peers.append(((y + dy) % NY) * 2 + (c + dc) % 2)
    barrier = pltpu.get_barrier_semaphore()
    for mm in peers:
        pl.semaphore_signal(barrier, inc=1, device_id={"rows": z * NM + mm}, device_id_type=MESH)
    for dz in (1, -1, 3, -3):
        pl.semaphore_signal(barrier, inc=1, device_id=z_dev(dz), device_id_type=MESH)
    for ds in (1, 2, 3):
        pl.semaphore_signal(
            barrier, inc=1, device_id={"src": (me_src + ds) % NSRC}, device_id_type=MESH
        )

    for b in range(4):
        zin[b, 0, 16:48] = jnp.zeros((32, B), BF16)
    for h in range(2):
        for s in range(ROWS_DEV):
            low[h, s] = misfit[pl.ds(s * SRC + h * HALF, HALF), :].astype(BF16)
    load_u.wait()
    load_v.wait()
    pl.semaphore_wait(barrier, len(peers) + 4 + NSRC - 1)

    order = peers + [m]
    lane = lax.broadcasted_iota(jnp.int32, (HALF, RMAX), 1)

    def y_copy(ph, p, i):
        return pltpu.make_async_remote_copy(
            src_ref=send.at[ph % 2, p, i],
            dst_ref=recv.at[ph % 4, p, m],
            send_sem=send_sem.at[ph % 2, p, i],
            recv_sem=recv_sem.at[ph % 4, p, m],
            device_id={"rows": z * NM + order[i]},
            device_id_type=MESH,
        )

    def y_arrival(ph, p, i):
        return pltpu.make_async_remote_copy(
            src_ref=send.at[ph % 2, p, i],
            dst_ref=recv.at[ph % 4, p, order[i]],
            send_sem=send_sem.at[ph % 2, p, i],
            recv_sem=recv_sem.at[ph % 4, p, order[i]],
            device_id={"rows": z * NM + order[i]},
            device_id_type=MESH,
        )

    def compute(ph, p):
        h = ph % 2

        @pl.when(ph >= 2)
        def _():
            for i in range(NM - 1):
                y_copy(ph, p, i).wait_send()

        layers = [(z + off) % NZ for off in offsets_of(p)]
        for i in range(NM):
            for q in range(2):
                d = layers[q] * NM + order[i]
                j = tab[0, d]
                acc = lax.dot_general(
                    low[h, tab[1, d]], u[j], CONTRACT_LAST, preferred_element_type=F32
                )
                coeff[i, q] = jnp.where(lane < tab[2, d], acc, 0.0)
        for i in range(NM):
            terms = []
            for q in range(2):
                d = layers[q] * NM + order[i]
                terms.append(
                    jnp.dot(
                        coeff[i, q].astype(BF16), v[tab[0, d]], preferred_element_type=F32
                    )
                )
            block = jnp.concatenate(terms, axis=0).astype(BF16)
            if i < NM - 1:
                send[h, p, i] = block
                y_copy(ph, p, i).start()
            else:
                recv[ph % 4, p, m] = block

    def z_full(ph, p, way):
        rows = pl.ds(way * 32, 32)
        return pltpu.make_async_remote_copy(
            src_ref=zs.at[ph % 2, p, rows],
            dst_ref=zin.at[ph % 4, p, rows],
            send_sem=zs_sem.at[ph % 2, p, way],
            recv_sem=zr_sem.at[ph % 4, p, way],
            device_id=z_dev((1 - 2 * way) * (3 - 2 * (p % 2))),
            device_id_type=MESH,
        )

    def z_first(ph, way):
        return pltpu.make_async_remote_copy(
            src_ref=zs.at[ph % 2, 0, pl.ds(way * 16, 16)],
            dst_ref=zin.at[ph % 4, 0, pl.ds(way * 48, 16)],
            send_sem=zs_sem.at[ph % 2, 0, way],
            recv_sem=zr_sem.at[ph % 4, 0, way],
            device_id=z_dev(1 - 2 * way),
            device_id_type=MESH,
        )

    def reduce(ph, p):
        h = ph % 2
        for i in range(NM - 1):
            y_arrival(ph, p, i).wait_recv()

        def y_sums(cols):
            got = recv[ph % 4, p, :, :, cols].reshape(NM * SRC, CHUNK)
            return jnp.dot(onehot[p], got, preferred_element_type=F32)

        @pl.when(p == 0)
        def _():
            @pl.when(ph >= 2)
            def _():
                for way in range(2):
                    z_first(ph, way).wait_send()

            for ch in range(B // CHUNK):
                cols = pl.ds(ch * CHUNK, CHUNK)
                acc = y_sums(cols)
                zs[h, 0, 0:32, cols] = acc[0:32].astype(BF16)
                own[h, :, cols] = acc[32:64]
            for way in range(2):
                z_first(ph, way).start()

        @pl.when(p > 0)
        def _():
            @pl.when(ph >= 2)
            def _():
                for way in range(2):
                    z_full(ph, p, way).wait_send()

            @pl.when(p == 2)
            def _():
                for way in range(2):
                    z_first(ph, way).wait_recv()

            @pl.when(p == 3)
            def _():
                for way in range(2):
                    z_full(ph, 1, way).wait_recv()

            @pl.when(p == 1)
            def _():
                for ch in range(B // CHUNK):
                    cols = pl.ds(ch * CHUNK, CHUNK)
                    zs[h, p, :, cols] = y_sums(cols).astype(BF16)

            @pl.when(p > 1)
            def _():
                for ch in range(B // CHUNK):
                    cols = pl.ds(ch * CHUNK, CHUNK)
                    acc = y_sums(cols) + zin[ph % 4, p - 2, :, cols].astype(F32)
                    zs[h, p, :, cols] = acc.astype(BF16)

            for way in range(2):
                z_full(ph, p, way).start()

    def finish(ph):
        h = ph % 2
        for p in (2, 3):
            for way in range(2):
                z_full(ph, p, way).wait_recv()
        for ch in range(B // CHUNK):
            cols = pl.ds(ch * CHUNK, CHUNK)
            arrived = zin[ph % 4, 2, :, cols].astype(F32) + zin[ph % 4, 3, :, cols].astype(F32)
            total = own[h, :, cols] + arrived[0:32] + arrived[32:64]
            for s in range(ROWS_DEV):
                rows = pl.ds(pl.multiple_of(s * SRC + h * HALF, HALF), HALF)
                value = (
                    misfit[rows, cols]
                    + contrast[pl.ds(s, 1), cols] * total[s * HALF : (s + 1) * HALF]
                )
                field_ref[rows, cols] = value
                low[h, s, :, cols] = value.astype(BF16)

    steps = 2 * APPS * 4

    def step(g, carry):
        @pl.when(g < steps)
        def _():
            compute(g // 4, g % 4)

        @pl.when(g >= LAG)
        def _():
            back = g - LAG
            reduce(back // 4, back % 4)

        @pl.when((g % 4 == 3) & (g >= 7))
        def _():
            finish(g // 4 - 1)

        return carry

    lax.fori_loop(0, steps + LAG, step, 0)
    finish(2 * APPS - 1)

    for ph in (2 * APPS - 2, 2 * APPS - 1):
        for p in range(4):
            for i in range(NM - 1):
                y_copy(ph, p, i).wait_send()
            for way in range(2):
                (z_full(ph, p, way) if p else z_first(ph, way)).wait_send()

    for s in range(ROWS_DEV):
        rows = pl.ds(s * SRC, SRC)
        product = forward[rows, :].astype(F32) * field_ref[rows, :]
        gbuf[0, pl.ds(s, 1), :] = jnp.sum(product, axis=0, keepdims=True)

    def g_copy(ds):
        return pltpu.make_async_remote_copy(
            src_ref=gbuf.at[0],
            dst_ref=gbuf.at[ds],
            send_sem=gs_sem.at[ds],
            recv_sem=gr_sem.at[ds],
            device_id={"src": (me_src + ds) % NSRC},
            device_id_type=MESH,
        )

    for ds in (1, 2, 3):
        g_copy(ds).start()
    for ds in (1, 2, 3):
        g_copy(ds).wait()
    even = (gbuf[0] + gbuf[2], gbuf[1] + gbuf[3])
    grad_ref[...] = (even[0] + even[1]) * (NSRC * SRC) ** -0.5


def tables(ranks, tile_cols, owner_slot):
    here = lax.axis_index("rows")
    z, m = here // NM, here % NM
    plane = lax.dynamic_slice_in_dim(tile_cols.reshape(NZ, NM, TILES), z, 1, 0)[0]
    slots = jnp.arange(owner_slot.shape[0], dtype=jnp.int32)
    target = jnp.sum(jnp.where(plane[:, :, None] == slots, owner_slot, 0), axis=2)
    target_dev, local = target // ROWS_DEV, target % ROWS_DEV
    mine = lax.dynamic_index_in_dim(target_dev, m, 0, keepdims=False)
    goes = mine[None, :] == jnp.arange(PEERS, dtype=jnp.int32)[:, None]
    tiles = jnp.arange(TILES, dtype=jnp.int32)
    values = jnp.stack([tiles, tiles // K, ranks.reshape(TILES)])
    tab = jnp.sum(jnp.where(goes[None], values[:, None, :], 0), axis=2)
    layer = jnp.concatenate([z + off for off in offsets_of(jnp.arange(4, dtype=jnp.int32))])
    dest = (layer % NZ) * NM + m
    comes = target_dev[None] == dest[:, None, None]
    q = jnp.sum(jnp.where(comes, local[None], 0), axis=2).reshape(2, 4, NM)
    row = jnp.arange(TILES, dtype=jnp.int32)[:, None]
    col = jnp.arange(NM * SRC, dtype=jnp.int32)[None, :]
    same = ((row % HALF) == (col % HALF)) & ((row // 32) == (col // HALF % 2))
    slot = jnp.repeat(q, SRC, axis=2)
    slot = jnp.where((row // 32)[None] == 0, slot[0][:, None, :], slot[1][:, None, :])
    onehot = (slot == (row // HALF % ROWS_DEV)[None]) & same[None]
    return tab.astype(jnp.int32), onehot.astype(BF16)


def per_device(
    misfit, forward_fields, contrast, u_factors, v_factors, ranks, tile_cols, owner_slot
):
    tab, onehot = tables(ranks, tile_cols, owner_slot)
    vmem = pl.BlockSpec(memory_space=pltpu.VMEM)
    hbm = pl.BlockSpec(memory_space=pl.ANY)
    dma = pltpu.SemaphoreType.DMA
    field, gradient = pl.pallas_call(
        kernel,
        out_shape=(
            jax.ShapeDtypeStruct((TILES, B), F32),
            jax.ShapeDtypeStruct((ROWS_DEV, B), F32),
        ),
        in_specs=[pl.BlockSpec(memory_space=pltpu.SMEM), vmem, vmem, vmem, vmem, hbm, hbm],
        out_specs=(vmem, vmem),
        scratch_shapes=[
            pltpu.VMEM((TILES, RMAX, B), BF16),
            pltpu.VMEM((TILES, RMAX, B), BF16),
            pltpu.VMEM((2, ROWS_DEV, HALF, B), BF16),
            pltpu.VMEM((NM, 2, HALF, RMAX), F32),
            pltpu.VMEM((2, 4, NM - 1, SRC, B), BF16),
            pltpu.VMEM((4, 4, NM, SRC, B), BF16),
            pltpu.VMEM((2, 4, TILES, B), BF16),
            pltpu.VMEM((4, 4, TILES, B), BF16),
            pltpu.VMEM((2, 32, B), F32),
            pltpu.VMEM((NSRC, ROWS_DEV, B), F32),
            dma((2,)),
            dma((2, 4, NM - 1)),
            dma((4, 4, NM)),
            dma((2, 4, 2)),
            dma((4, 4, 2)),
            dma((NSRC,)),
            dma((NSRC,)),
        ],
        compiler_params=pltpu.CompilerParams(
            collective_id=0, has_side_effects=True, vmem_limit_bytes=58 * 1024 * 1024
        ),
    )(
        tab,
        misfit.reshape(TILES, B),
        forward_fields.reshape(TILES, B),
        contrast,
        onehot,
        u_factors.reshape(TILES, RMAX, B),
        v_factors.reshape(TILES, RMAX, B),
    )
    return field.reshape(ROWS_DEV, SRC, B), gradient


def solution(mesh):
    placed = (
        P("rows", "src", None),
        P("rows", "src", None),
        P("rows", None),
        P("rows", None, None, None),
        P("rows", None, None, None),
        P("rows", None),
        P(),
        P(),
    )
    return jax.shard_map(
        per_device,
        mesh=mesh,
        in_specs=placed,
        out_specs=(P("rows", "src", None), P("rows", None)),
        check_vma=False,
    )
```

```python
import jax
import jax.numpy as jnp
from jax import lax
from jax.experimental import pallas as pl
from jax.experimental.pallas import tpu as pltpu
from jax.sharding import PartitionSpec as P

B = 1024
K = 16
RMAX = 96
APPS = 4
ROWS_DEV = 4
TILES = ROWS_DEV * K
NZ = 8
NY = 4
NM = 8
SRC = 16
PEERS = NZ * NM
NSRC = 4
MESH = pl.DeviceIdType.MESH
CONTRACT_LAST = (((1,), (1,)), ((), ()))
F32 = jnp.float32
BF16 = jnp.bfloat16
CHUNK = 256
HALF = 8
LAG = 2
CODE = 128


def offsets_of(p):
    far = 4 - 2 * p + 3 * (p // 2)
    return far, jnp.minimum(p, 1) * (NZ - far)


def kernel(
    tab,
    misfit,
    forward,
    contrast,
    slot_of,
    u_hbm,
    v_hbm,
    field_ref,
    grad_ref,
    u,
    v,
    low,
    coeff,
    send,
    recv,
    zs,
    zin,
    own,
    onehot,
    gbuf,
    load_sem,
    send_sem,
    recv_sem,
    zs_sem,
    zr_sem,
    gs_sem,
    gr_sem,
):
    here = lax.axis_index("rows")
    me_src = lax.axis_index("src")
    z = here // NM
    m = here % NM
    y = m // 2
    c = m % 2

    def load(n):
        tiles = pl.ds(n % 2 * (TILES // 2), TILES // 2)
        src, dst = ((u_hbm, u), (v_hbm, v))[n // 2]
        return pltpu.make_async_copy(src.at[tiles], dst.at[tiles], load_sem.at[n])

    load(0).start()
    load(1).start()

    def z_dev(dz):
        return {"rows": ((z + NZ + dz) % NZ) * NM + m}

    peers = []
    for dy in (2, 1, 3, 0):
        for dc in (0, 1):
            if dy or dc:
                peers.append(((y + dy) % NY) * 2 + (c + dc) % 2)
    barrier = pltpu.get_barrier_semaphore()
    for mm in peers:
        pl.semaphore_signal(barrier, inc=1, device_id={"rows": z * NM + mm}, device_id_type=MESH)
    for dz in (1, -1, 3, -3):
        pl.semaphore_signal(barrier, inc=1, device_id=z_dev(dz), device_id_type=MESH)
    for ds in (1, 2, 3):
        pl.semaphore_signal(
            barrier, inc=1, device_id={"src": (me_src + ds) % NSRC}, device_id_type=MESH
        )

    for b in range(4):
        zin[b, 0, 16:48] = jnp.zeros((32, B), BF16)
    for h in range(2):
        for s in range(ROWS_DEV):
            low[h, s] = misfit[pl.ds(s * SRC + h * HALF, HALF), :].astype(BF16)
    row = lax.broadcasted_iota(jnp.int32, (TILES, NM * SRC), 0)
    col = lax.broadcasted_iota(jnp.int32, (TILES, NM * SRC), 1)
    same = ((row % HALF) == (col % HALF)) & ((row // 32) == (col // HALF % 2))
    for p in range(4):
        slot = jnp.zeros((TILES, NM * SRC), jnp.int32)
        for half in range(2):
            for mm in range(NM):
                where = (col // SRC == mm) & (row // 32 == half)
                slot = jnp.where(where, slot_of[half * 32 + p * NM + mm], slot)
        hit = same & (slot == row // HALF % ROWS_DEV)
        onehot[p] = jnp.where(hit, 1.0, 0.0).astype(BF16)
    load(0).wait()
    load(2).start()
    load(1).wait()
    load(3).start()

    order = peers + [m]
    lane = lax.broadcasted_iota(jnp.int32, (HALF, RMAX), 1)

    def y_copy(ph, p, i):
        return pltpu.make_async_remote_copy(
            src_ref=send.at[ph % 2, p, i],
            dst_ref=recv.at[ph % 4, p, m],
            send_sem=send_sem.at[ph % 2, p, i],
            recv_sem=recv_sem.at[ph % 4, p, m],
            device_id={"rows": z * NM + order[i]},
            device_id_type=MESH,
        )

    def y_arrival(ph, p, i):
        return pltpu.make_async_remote_copy(
            src_ref=send.at[ph % 2, p, i],
            dst_ref=recv.at[ph % 4, p, order[i]],
            send_sem=send_sem.at[ph % 2, p, i],
            recv_sem=recv_sem.at[ph % 4, p, order[i]],
            device_id={"rows": z * NM + order[i]},
            device_id_type=MESH,
        )

    def layers_of(p):
        return [(z + off) % NZ for off in offsets_of(p)]

    def coefficients(ph, p):
        h = ph % 2
        layers = layers_of(p)
        for i in range(NM):
            for q in range(2):
                d = layers[q] * NM + order[i]
                code = tab[d]
                j = code // CODE
                acc = lax.dot_general(
                    low[h, code // (CODE * K)], u[j], CONTRACT_LAST, preferred_element_type=F32
                )
                coeff[i, q] = jnp.where(lane < code % CODE, acc, 0.0)

    def send_terms(ph, p):
        h = ph % 2
        layers = layers_of(p)
        for i in range(NM):
            terms = []
            for q in range(2):
                d = layers[q] * NM + order[i]
                terms.append(
                    jnp.dot(
                        coeff[i, q].astype(BF16), v[tab[d] // CODE], preferred_element_type=F32
                    )
                )
            block = jnp.concatenate(terms, axis=0).astype(BF16)
            if i < NM - 1:
                send[h, p, i] = block
                y_copy(ph, p, i).start()
            else:
                recv[ph % 4, p, m] = block

    def z_full(ph, p, way):
        rows = pl.ds(way * 32, 32)
        return pltpu.make_async_remote_copy(
            src_ref=zs.at[ph % 2, p, rows],
            dst_ref=zin.at[ph % 4, p, rows],
            send_sem=zs_sem.at[ph % 2, p, way],
            recv_sem=zr_sem.at[ph % 4, p, way],
            device_id=z_dev((1 - 2 * way) * (3 - 2 * (p % 2))),
            device_id_type=MESH,
        )

    def z_first(ph, way):
        return pltpu.make_async_remote_copy(
            src_ref=zs.at[ph % 2, 0, pl.ds(way * 16, 16)],
            dst_ref=zin.at[ph % 4, 0, pl.ds(way * 48, 16)],
            send_sem=zs_sem.at[ph % 2, 0, way],
            recv_sem=zr_sem.at[ph % 4, 0, way],
            device_id=z_dev(1 - 2 * way),
            device_id_type=MESH,
        )

    def reduce(ph, p):
        h = ph % 2
        for i in range(NM - 1):
            y_arrival(ph, p, i).wait_recv()

        def y_sums(cols):
            got = recv[ph % 4, p, :, :, cols].reshape(NM * SRC, CHUNK)
            return jnp.dot(onehot[p], got, preferred_element_type=F32)

        @pl.when(p == 0)
        def _():
            @pl.when(ph >= 2)
            def _():
                for way in range(2):
                    z_first(ph, way).wait_send()

            for ch in range(B // CHUNK):
                cols = pl.ds(ch * CHUNK, CHUNK)
                acc = y_sums(cols)
                zs[h, 0, 0:32, cols] = acc[0:32].astype(BF16)
                own[h, :, cols] = acc[32:64]
            for way in range(2):
                z_first(ph, way).start()

        @pl.when(p > 0)
        def _():
            @pl.when(ph >= 2)
            def _():
                for way in range(2):
                    z_full(ph, p, way).wait_send()

            @pl.when(p == 2)
            def _():
                for way in range(2):
                    z_first(ph, way).wait_recv()

            @pl.when(p == 3)
            def _():
                for way in range(2):
                    z_full(ph, 1, way).wait_recv()

            @pl.when(p == 1)
            def _():
                for ch in range(B // CHUNK):
                    cols = pl.ds(ch * CHUNK, CHUNK)
                    zs[h, p, :, cols] = y_sums(cols).astype(BF16)

            @pl.when(p > 1)
            def _():
                for ch in range(B // CHUNK):
                    cols = pl.ds(ch * CHUNK, CHUNK)
                    acc = y_sums(cols) + zin[ph % 4, p - 2, :, cols].astype(F32)
                    zs[h, p, :, cols] = acc.astype(BF16)

            for way in range(2):
                z_full(ph, p, way).start()

    def finish(ph):
        h = ph % 2
        for p in (2, 3):
            for way in range(2):
                z_full(ph, p, way).wait_recv()
        for ch in range(B // CHUNK):
            cols = pl.ds(ch * CHUNK, CHUNK)
            arrived = zin[ph % 4, 2, :, cols].astype(F32) + zin[ph % 4, 3, :, cols].astype(F32)
            total = own[h, :, cols] + arrived[0:32] + arrived[32:64]
            for s in range(ROWS_DEV):
                rows = pl.ds(pl.multiple_of(s * SRC + h * HALF, HALF), HALF)
                value = (
                    misfit[rows, cols]
                    + contrast[pl.ds(s, 1), cols] * total[s * HALF : (s + 1) * HALF]
                )
                field_ref[rows, cols] = value
                low[h, s, :, cols] = value.astype(BF16)

    steps = 2 * APPS * 4

    def step(g, carry):
        @pl.when(g < steps)
        def _():
            ph, p = g // 4, g % 4

            @pl.when(ph >= 2)
            def _():
                for i in range(NM - 1):
                    y_copy(ph, p, i).wait_send()

            coefficients(ph, p)
            send_terms(ph, p)

        @pl.when(g >= LAG)
        def _():
            back = g - LAG
            reduce(back // 4, back % 4)

        @pl.when((g % 4 == 3) & (g >= 7))
        def _():
            finish(g // 4 - 1)

        return carry

    coefficients(jnp.int32(0), jnp.int32(0))
    load(2).wait()
    load(3).wait()
    pl.semaphore_wait(barrier, len(peers) + 4 + NSRC - 1)
    send_terms(jnp.int32(0), jnp.int32(0))
    lax.fori_loop(1, steps + LAG, step, 0)
    finish(2 * APPS - 1)

    for ph in (2 * APPS - 2, 2 * APPS - 1):
        for p in range(4):
            for i in range(NM - 1):
                y_copy(ph, p, i).wait_send()
            for way in range(2):
                (z_full(ph, p, way) if p else z_first(ph, way)).wait_send()

    for s in range(ROWS_DEV):
        rows = pl.ds(s * SRC, SRC)
        product = forward[rows, :].astype(F32) * field_ref[rows, :]
        gbuf[0, pl.ds(s, 1), :] = jnp.sum(product, axis=0, keepdims=True)

    def g_copy(ds):
        return pltpu.make_async_remote_copy(
            src_ref=gbuf.at[0],
            dst_ref=gbuf.at[ds],
            send_sem=gs_sem.at[ds],
            recv_sem=gr_sem.at[ds],
            device_id={"src": (me_src + ds) % NSRC},
            device_id_type=MESH,
        )

    for ds in (1, 2, 3):
        g_copy(ds).start()
    for ds in (1, 2, 3):
        g_copy(ds).wait()
    even = (gbuf[0] + gbuf[2], gbuf[1] + gbuf[3])
    grad_ref[...] = (even[0] + even[1]) * (NSRC * SRC) ** -0.5


def tables(ranks, tile_cols, owner_slot):
    here = lax.axis_index("rows")
    z, m = here // NM, here % NM
    plane = lax.dynamic_slice_in_dim(tile_cols, z * NM * ROWS_DEV, NM * ROWS_DEV, 0)
    slots = jnp.arange(owner_slot.shape[0], dtype=jnp.int32)
    target = jnp.sum(jnp.where(plane[:, :, None] == slots, owner_slot, 0), axis=2)
    target_dev, local = target // ROWS_DEV, target % ROWS_DEV
    mine = lax.dynamic_slice_in_dim(target_dev, m * ROWS_DEV, ROWS_DEV, 0)
    goes = mine[None] == jnp.arange(PEERS, dtype=jnp.int32)[:, None, None]
    tile = lax.broadcasted_iota(jnp.int32, (ROWS_DEV, K), 0) * K
    tile = tile + lax.broadcasted_iota(jnp.int32, (ROWS_DEV, K), 1)
    tab = jnp.sum(jnp.where(goes, (tile * CODE + ranks)[None], 0), axis=(1, 2))
    layer = jnp.concatenate([z + off for off in offsets_of(jnp.arange(4, dtype=jnp.int32))])
    dest = (layer % NZ) * NM + m
    comes = target_dev[None] == dest[:, None, None]
    q = jnp.sum(jnp.where(comes, local[None], 0), axis=2)
    q = jnp.sum(q.reshape(PEERS, ROWS_DEV), axis=1)
    return tab, q


def place_kernel(field_in, grad_in, field_out, grad_out):
    field_out[...] = field_in[...]
    grad_out[...] = grad_in[...]


def per_device(
    misfit, forward_fields, contrast, u_factors, v_factors, ranks, tile_cols, owner_slot
):
    tab, slot_of = tables(ranks, tile_cols, owner_slot)
    vmem = pl.BlockSpec(memory_space=pltpu.VMEM)
    smem = pl.BlockSpec(memory_space=pltpu.SMEM)
    hbm = pl.BlockSpec(memory_space=pl.ANY)
    dma = pltpu.SemaphoreType.DMA
    field, gradient = pl.pallas_call(
        kernel,
        out_shape=(
            jax.ShapeDtypeStruct((TILES, B), F32),
            jax.ShapeDtypeStruct((ROWS_DEV, B), F32),
        ),
        in_specs=[smem, vmem, vmem, vmem, smem, hbm, hbm],
        out_specs=(vmem, vmem),
        scratch_shapes=[
            pltpu.VMEM((TILES, RMAX, B), BF16),
            pltpu.VMEM((TILES, RMAX, B), BF16),
            pltpu.VMEM((2, ROWS_DEV, HALF, B), BF16),
            pltpu.VMEM((NM, 2, HALF, RMAX), F32),
            pltpu.VMEM((2, 4, NM - 1, SRC, B), BF16),
            pltpu.VMEM((4, 4, NM, SRC, B), BF16),
            pltpu.VMEM((2, 4, TILES, B), BF16),
            pltpu.VMEM((4, 4, TILES, B), BF16),
            pltpu.VMEM((2, 32, B), F32),
            pltpu.VMEM((4, TILES, NM * SRC), BF16),
            pltpu.VMEM((NSRC, ROWS_DEV, B), F32),
            dma((4,)),
            dma((2, 4, NM - 1)),
            dma((4, 4, NM)),
            dma((2, 4, 2)),
            dma((4, 4, 2)),
            dma((NSRC,)),
            dma((NSRC,)),
        ],
        compiler_params=pltpu.CompilerParams(
            collective_id=0, has_side_effects=True, vmem_limit_bytes=58 * 1024 * 1024
        ),
    )(
        tab,
        misfit.reshape(TILES, B),
        forward_fields.reshape(TILES, B),
        contrast,
        slot_of,
        u_factors.reshape(TILES, RMAX, B),
        v_factors.reshape(TILES, RMAX, B),
    )
    field, gradient = pl.pallas_call(
        place_kernel,
        out_shape=(
            jax.ShapeDtypeStruct((TILES, B), F32),
            jax.ShapeDtypeStruct((ROWS_DEV, B), F32),
        ),
        in_specs=[vmem, vmem],
        out_specs=(vmem, vmem),
    )(field, gradient)
    return field.reshape(ROWS_DEV, SRC, B), gradient


def solution(mesh):
    placed = (
        P("rows", "src", None),
        P("rows", "src", None),
        P("rows", None),
        P("rows", None, None, None),
        P("rows", None, None, None),
        P("rows", None),
        P(),
        P(),
    )
    return jax.shard_map(
        per_device,
        mesh=mesh,
        in_specs=placed,
        out_specs=(P("rows", "src", None), P("rows", None)),
        check_vma=False,
    )
```
